32 devices in a mesh: dev: 32 (over z, y, x, core).
Axes of the slice: x: 2, y: 2, z: 4, core: 2. Of those that a mesh axis runs over, the one named last changes fastest.
Arguments:
- conductivity: float32 [128, 3, 2048], P('dev'), may hold values from 0.05 to 1
- block_ids: int32 [64, 16], P('dev'), may hold values from 0 to 127, as said below
- weights: int32 [64, 8], P('dev'), may hold values from 1 to 7
- source: float32 [64, 3, 8, 16, 128], P('dev'), may hold values from -6 to 6
- cotangent: float32 [64, 3, 8, 16, 128], P('dev'), may hold values from -6 to 6
Outputs:
- fields: float32 [64, 3, 8, 16, 128], P('dev')
- gradient: float32 [128, 3, 2048], P('dev')
The draws below stay inside these ranges and needn't reach their ends.
Inputs may be any that keep to these rules, and one draw needn't show every extreme that they name: `block_ids`: the 32 entries of the meshes of one device (an aligned block of 2 rows) name blocks of all owners, each owner exactly once, the owner of a block being its id // 4.
All inputs are finite; a program needn't handle non-finite values.
Results may differ from the reference program's by a relative error of at most 0.00002.
Values sent between devices are 32-bit elements; how exact they have to be, the bound alone decides.
No kernel may reach another device: no remote copies, remote signals or barrier semaphores. Data moves between devices by JAX's collectives and lax.ppermute only.
A program may use at most 128 MiB of HBM per device.

```python
import math
import jax
import jax.numpy as jnp
from jax import lax

MX = 8
MY = 16
MZ = 128
STEPS = 10
BLK_DEV = 4
MESH_DEV = 2
BC = 2048
NBLK = 128
MESHES = 64
N_DEV = 32


def draw_block_ids(key, part):
    entry_count = MESH_DEV * 2 * MX

    def per_device(device_number):
        device_key = jax.random.fold_in(key, device_number)
        owners = jax.random.permutation(jax.random.fold_in(device_key, 11), N_DEV)[:entry_count]
        local_rows = jax.random.randint(jax.random.fold_in(device_key, 23), (entry_count,), 0, BLK_DEV)
        return (owners * BLK_DEV + local_rows).reshape(MESH_DEV, 2 * MX)
    table = jax.vmap(per_device)(jnp.arange(N_DEV))
    return table.reshape(MESH_DEV * N_DEV, 2 * MX).astype(jnp.int32)


def plant(array, rng, low, largest):
    place = [jax.random.randint(jax.random.fold_in(rng, axis), (), 0, length) for axis, length in enumerate(array.shape)]
    longest = array.shape.index(max(array.shape))
    next_to = place[:longest] + [(place[longest] + 1) % array.shape[longest]] + place[longest + 1:]
    return array.at[tuple(place)].set(low).at[tuple(next_to)].set(largest)


def level_of(rng, shape, split, least, top_value):
    level = 1.0
    for axis_at, parts in split:
        heights = jax.random.uniform(jax.random.fold_in(jax.random.fold_in(rng, 6), axis_at), (parts,), jnp.float32, least / len(split), top_value / len(split))
        level = level * jnp.repeat(jnp.exp(heights), shape[axis_at] // parts).reshape((-1,) + (1,) * (len(shape) - 1 - axis_at))
    return level


def normal_values(stream_key, shape, deviation, limit, pieces=(), held_as=jnp.bfloat16):
    factor_of = level_of(stream_key, shape, pieces, -0.22, 0.18) if pieces else 1.0
    array = jax.random.normal(stream_key, shape, jnp.float32) * deviation * factor_of
    return jnp.minimum(jnp.maximum(array, -limit), limit).astype(held_as)


def setup_inputs(seed: int = 0) -> dict:
    streams_of = jax.random.split(jax.random.key(seed), 6)
    return {
        "conductivity": jnp.clip(jnp.exp(math.log(1.0) - 2.9957323 * jax.random.uniform(streams_of[0], (NBLK, 3, BC), jnp.float32) ** level_of(streams_of[0], (NBLK, 3, BC), ((0, 32),), -0.2, 0.2)), 0.05, 1.0),
        "block_ids": draw_block_ids(jax.random.fold_in(streams_of[5], 71), 0),
        "weights": plant(jax.random.randint(streams_of[2], (MESHES, MX), 1, 8), jax.random.fold_in(streams_of[2], 1), 1, 7).astype(jnp.int32),
        "source": normal_values(streams_of[3], (MESHES, 3, MX, MY, MZ), 1.0, 6.0, ((0, 32),), jnp.float32),
        "cotangent": normal_values(streams_of[4], (MESHES, 3, MX, MY, MZ), 1.0, 6.0, ((0, 32),), jnp.float32),
    }


time_step = 0.5

def difference(values, direction, forward):
    length = values.shape[direction]
    zero_plane = jnp.zeros_like(lax.slice_in_dim(values, 0, 1, axis=direction))
    if forward:
        later = jnp.concatenate([lax.slice_in_dim(values, 1, length, axis=direction), zero_plane], axis=direction)
        return later - values
    earlier = jnp.concatenate([zero_plane, lax.slice_in_dim(values, 0, length - 1, axis=direction)], axis=direction)
    return values - earlier

def curl_of(vector, forward):
    first = difference(vector[2], 1, forward) - difference(vector[1], 2, forward)
    second = difference(vector[0], 2, forward) - difference(vector[2], 0, forward)
    third = difference(vector[1], 0, forward) - difference(vector[0], 1, forward)
    return jnp.stack([first, second, third])

def evolve(damping, initial):

    def leapfrog(state_pair, unused_item):
        electric, magnetic = state_pair
        magnetic = magnetic - time_step * curl_of(electric, True)
        electric = electric + time_step * (curl_of(magnetic, False) - damping * electric)
        return ((electric, magnetic), None)
    final_pair, unused_out = lax.scan(leapfrog, (initial, jnp.zeros_like(initial)), None, length=STEPS)
    return final_pair[0]

def mesh_field(picked, mesh_weights, initial):
    fraction = mesh_weights.astype(jnp.float32) / 8.0
    near_part = picked[:MX]
    far_part = picked[MX:]
    damping = fraction[:, None, None] * near_part + (1.0 - fraction)[:, None, None] * far_part
    damping = jnp.swapaxes(damping, 0, 1).reshape(3, MX, MY, MZ)
    return evolve(damping, initial)

def reference(conductivity, block_ids, weights, source, cotangent):

    def single_mesh(mesh_items):
        mesh_ids, mesh_weights, mesh_source, mesh_cotangent = mesh_items
        picked = conductivity[mesh_ids]
        electric, pullback = jax.vjp(lambda blocks_in: mesh_field(blocks_in, mesh_weights, mesh_source), picked)
        mesh_grads, = pullback(mesh_cotangent)
        return (electric, mesh_grads)
    fields, grads = lax.map(single_mesh, (block_ids, weights, source, cotangent))
    flat_ids = block_ids.reshape(-1).astype(jnp.int32)
    gradient = jnp.zeros_like(conductivity).at[flat_ids].add(grads.reshape(flat_ids.shape[0], 3, MY * MZ))
    return (fields, gradient)
```

```python
import functools

import jax
import jax.numpy as jnp
from jax import lax
from jax.experimental import pallas as pl
from jax.experimental.pallas import tpu as pltpu
from jax.sharding import PartitionSpec as P

STEPS = 10
ANY = pl.BlockSpec(memory_space=pl.ANY)
VMEM = pl.BlockSpec(memory_space=pltpu.VMEM)
SMEM = pl.BlockSpec(memory_space=pltpu.SMEM)


def request_kernel(count, blocks_here, ids_ref, out_ref):
    entries = ids_ref.shape[1]

    def one(entry, carry):
        block = ids_ref[entry // entries, entry % entries]
        out_ref[block // blocks_here, 0, 0] = block % blocks_here
        return carry

    lax.fori_loop(0, count, one, 0, unroll=8)


def gather_kernel(count, blocks_here, wanted_ref, rows_ref, out_ref):
    rows = out_ref.shape[1]
    for peer in range(count):
        row = wanted_ref[peer, 0, 0]
        out_ref[peer] = rows_ref[pl.ds(row, rows, stride=blocks_here), :]


def scatter_kernel(count, blocks_here, wanted_ref, in_ref, out_ref, total):
    rows = in_ref.shape[1]
    total[...] = jnp.zeros_like(total)
    for peer in range(count):
        row = wanted_ref[peer, 0, 0]
        total[row] = total[row] + in_ref[peer]
    for block in range(blocks_here):
        out_ref[pl.ds(block, rows, stride=blocks_here), :] = total[block]


def mesh_kernel(
    blocks_here,
    ids_ref,
    weights_ref,
    arrived_ref,
    source_ref,
    cotangent_ref,
    fields_ref,
    grads_ref,
    history,
    magnetic,
    keep,
    in_sem,
    out_sem,
):
    meshes = source_ref.shape[0]
    layers, height, width = source_ref.shape[2:]
    slots = history.shape[0]
    parts = 3

    def incoming(mesh, slot):
        return [
            pltpu.make_async_copy(ref.at[mesh], history.at[slot, run, 0], in_sem.at[slot, run])
            for run, ref in enumerate((source_ref, cotangent_ref))
        ]

    def outgoing(mesh, slot):
        return pltpu.make_async_copy(
            history.at[slot, 0, STEPS], fields_ref.at[mesh], out_sem.at[slot]
        )

    for mesh in range(slots):
        for copy in incoming(mesh, mesh):
            copy.start()

    lane = lax.broadcasted_iota(jnp.int32, (height, width), 1)
    line = lax.broadcasted_iota(jnp.int32, (height, width), 0)
    last_lane, first_lane = lane == width - 1, lane == 0
    last_line, first_line = line == height - 1, line == 0

    def plus_z(v):
        return jnp.where(last_lane, 0.0, pltpu.roll(v, width - 1, 1)) - v

    def plus_y(v):
        return jnp.where(last_line, 0.0, pltpu.roll(v, height - 1, 0)) - v

    def minus_z(v):
        return v - jnp.where(first_lane, 0.0, pltpu.roll(v, 1, 1))

    def minus_y(v):
        return v - jnp.where(first_line, 0.0, pltpu.roll(v, 1, 0))

    def sweep(slot, step, runs):
        for run in runs:
            now = [history[slot, run, step, c, 0] for c in range(parts)]
            below = None
            for layer in range(layers):
                ex, ey, ez = now
                if layer + 1 < layers:
                    above = [history[slot, run, step, c, layer + 1] for c in range(parts)]
                    dx_y, dx_z = above[1] - ey, above[2] - ez
                else:
                    above = None
                    dx_y, dx_z = -ey, -ez
                gx = magnetic[run, 0, layer] - 0.25 * (plus_y(ez) - plus_z(ey))
                gy = magnetic[run, 1, layer] - 0.25 * (plus_z(ex) - dx_z)
                gz = magnetic[run, 2, layer] - 0.25 * (dx_y - plus_y(ex))
                magnetic[run, 0, layer] = gx
                magnetic[run, 1, layer] = gy
                magnetic[run, 2, layer] = gz
                if below is None:
                    bx_y, bx_z = gy, gz
                else:
                    bx_y, bx_z = gy - below[0], gz - below[1]
                below = (gy, gz)
                history[slot, run, step + 1, 0, layer] = keep[0, layer] * ex + (
                    minus_y(gz) - minus_z(gy)
                )
                history[slot, run, step + 1, 1, layer] = keep[1, layer] * ey + (
                    minus_z(gx) - bx_z
                )
                history[slot, run, step + 1, 2, layer] = keep[2, layer] * ez + (
                    bx_y - minus_y(gx)
                )
                now = above

    def one_mesh(mesh, carry):
        slot = lax.rem(mesh, slots)
        for layer in range(layers):
            fraction = weights_ref[mesh, layer].astype(jnp.float32) * 0.125
            near = ids_ref[mesh, layer] // blocks_here
            far = ids_ref[mesh, layer + layers] // blocks_here
            for c in range(parts):
                rows = pl.ds(c * height, height)
                keep[c, layer] = 1.0 - 0.5 * (
                    fraction * arrived_ref[near, rows] + (1.0 - fraction) * arrived_ref[far, rows]
                )
        magnetic[...] = jnp.zeros_like(magnetic)
        for copy in incoming(mesh, slot):
            copy.wait()

        @pl.when(mesh >= slots)
        def _():
            outgoing(mesh - slots, slot).wait()

        def step_of(step, inner):
            sweep(slot, step, (0, 1))
            return inner

        lax.fori_loop(0, STEPS - 1, step_of, 0)
        sweep(slot, STEPS - 1, (0,))
        outgoing(mesh, slot).start()
        for layer in range(layers):
            fraction = weights_ref[mesh, layer].astype(jnp.float32) * 0.125
            near = ids_ref[mesh, layer] // blocks_here
            far = ids_ref[mesh, layer + layers] // blocks_here
            for c in range(parts):
                rows = pl.ds(c * height, height)
                total = None
                for step in range(STEPS):
                    term = history[slot, 0, step, c, layer] * history[slot, 1, STEPS - 1 - step, c, layer]
                    total = term if total is None else total + term
                total = -0.5 * total
                grads_ref[near, rows] = fraction * total
                grads_ref[far, rows] = (1.0 - fraction) * total

        @pl.when(mesh + slots < meshes)
        def _():
            for copy in incoming(mesh + slots, slot):
                copy.start()

        return carry

    lax.fori_loop(0, meshes, one_mesh, 0)
    for mesh in range(meshes - slots, meshes):
        outgoing(mesh, mesh % slots).wait()


def local(conductivity, block_ids, weights, source, cotangent):
    blocks_here, parts, cells = conductivity.shape
    meshes, _, layers, height, width = source.shape
    count = lax.axis_size("dev")
    rows = parts * cells // width
    f32 = jnp.float32
    requested = pl.pallas_call(
        functools.partial(request_kernel, block_ids.size, blocks_here),
        out_shape=jax.ShapeDtypeStruct((count, 1, 1), jnp.int32),
        in_specs=[SMEM],
        out_specs=SMEM,
        name="requests",
    )(block_ids)
    wanted = lax.all_to_all(requested, "dev", split_axis=0, concat_axis=0, tiled=True)
    own_rows = (
        conductivity.reshape(blocks_here, rows, width).transpose(1, 0, 2).reshape(-1, width)
    )
    outgoing = pl.pallas_call(
        functools.partial(gather_kernel, count, blocks_here),
        out_shape=jax.ShapeDtypeStruct((count, rows, width), f32),
        in_specs=[SMEM, VMEM],
        out_specs=VMEM,
        compiler_params=pltpu.CompilerParams(vmem_limit_bytes=16 << 20),
        name="collect",
    )(wanted, own_rows)
    arrived = lax.all_to_all(outgoing, "dev", split_axis=0, concat_axis=0, tiled=True)
    slots = min(meshes, 2)
    fields, grads = pl.pallas_call(
        functools.partial(mesh_kernel, blocks_here),
        out_shape=(
            jax.ShapeDtypeStruct(source.shape, f32),
            jax.ShapeDtypeStruct((count, rows, width), f32),
        ),
        in_specs=[SMEM, SMEM, VMEM, ANY, ANY],
        out_specs=(ANY, VMEM),
        scratch_shapes=[
            pltpu.VMEM((slots, 2, STEPS + 1, parts, layers, height, width), f32),
            pltpu.VMEM((2, parts, layers, height, width), f32),
            pltpu.VMEM((parts, layers, height, width), f32),
            pltpu.SemaphoreType.DMA((slots, 2)),
            pltpu.SemaphoreType.DMA((slots,)),
        ],
        compiler_params=pltpu.CompilerParams(vmem_limit_bytes=32 << 20),
        name="leapfrog",
    )(block_ids, weights, arrived, source, cotangent)
    returned = lax.all_to_all(grads, "dev", split_axis=0, concat_axis=0, tiled=True)
    gradient = pl.pallas_call(
        functools.partial(scatter_kernel, count, blocks_here),
        out_shape=jax.ShapeDtypeStruct((rows * blocks_here, width), f32),
        in_specs=[SMEM, VMEM],
        out_specs=VMEM,
        scratch_shapes=[pltpu.VMEM((blocks_here, rows, width), f32)],
        compiler_params=pltpu.CompilerParams(vmem_limit_bytes=16 << 20),
        name="deposit",
    )(wanted, returned)
    gradient = gradient.reshape(rows, blocks_here, width).transpose(1, 0, 2)
    return fields, gradient.reshape(conductivity.shape)


def solution(mesh):
    placed = (
        P("dev", None, None),
        P("dev", None),
        P("dev", None),
        P("dev", None, None, None, None),
        P("dev", None, None, None, None),
    )
    return jax.shard_map(
        local,
        mesh=mesh,
        in_specs=placed,
        out_specs=(P("dev", None, None, None, None), P("dev", None, None)),
        check_vma=False,
    )
```

```python
import functools

import jax
import jax.numpy as jnp
from jax import lax
from jax.experimental import pallas as pl
from jax.experimental.pallas import tpu as pltpu
from jax.sharding import PartitionSpec as P


STEPS = 10
PARTS = 3
PLANE = 4
HBM = pl.BlockSpec(memory_space=pltpu.HBM)
VMEM = pl.BlockSpec(memory_space=pltpu.VMEM)
SMEM = pl.BlockSpec(memory_space=pltpu.SMEM)


def limit(mib):
    return pltpu.CompilerParams(vmem_limit_bytes=mib << 20)


def split_block(block, blocks_here):
    if blocks_here & (blocks_here - 1) == 0:
        shift = blocks_here.bit_length() - 1
        owner = lax.shift_right_logical(block, shift)
        return owner, block & (blocks_here - 1)
    owner = lax.div(block, blocks_here)
    return owner, block - owner * blocks_here


def offset(column, side, core):
    return (column * PLANE + side) * 2 + core


def fill_rows(ids_ref, blocks_here, table, *lead):
    meshes, entries = ids_ref.shape

    def one_mesh(mesh, carry):
        for entry in range(entries):
            owner, row = split_block(ids_ref[mesh, entry], blocks_here)
            table[(*lead, owner)] = row
        return carry

    lax.fori_loop(0, meshes, one_mesh, 0)


def copy_rows(table_ref, group, unit_refs, out_refs, blocks_here):
    rows = out_refs[0].shape[1]
    for place, column in enumerate(group):
        for core in range(2):
            for side in range(1, PLANE):
                row = table_ref[side, 2 * column + core]
                out_refs[side - 1][2 * place + core] = unit_refs[2 * place + core][
                    pl.ds(row, rows, stride=blocks_here), :
                ]


def lookup_kernel(columns, blocks_here, *refs):
    ids_refs, (table_ref, spread) = refs[:PLANE], refs[PLANE:]
    me = lax.axis_index("dev")
    for side in range(PLANE):
        fill_rows(ids_refs[side], blocks_here, spread, side)
    for side in range(PLANE):
        for column in range(columns):
            for core in range(2):
                owner = me ^ offset(column, 0, core)
                table_ref[side, 2 * column + core] = spread[side, owner]


def gather_kernel(group, blocks_here, table_ref, *refs):
    copy_rows(table_ref, group, refs[: 2 * len(group)], refs[2 * len(group) :], blocks_here)


def partner_kernel(group, core, table_ref, own_ref, *refs):
    in_refs, refs = refs[: PLANE - 1], refs[PLANE - 1 :]
    if core == 0:
        partner_ref, out_refs = refs[0], refs[1:]
    else:
        out_refs = refs
    for place, column in enumerate(group):
        out_ref = out_refs[place] if core == 0 else out_refs[0].at[place]
        if core == 0:
            out_ref[...] = partner_ref[place]
        else:
            out_ref[...] = jnp.zeros_like(out_ref)
        for side in range(PLANE):
            row = table_ref[side, 2 * column + core]
            if side == 0:
                value = own_ref[2 * column + core]
            else:
                value = in_refs[side - 1][2 * place + core]
            out_ref[row] = out_ref[row] + value


def final_kernel(*refs):
    in_refs, out_ref = refs[:-1], refs[-1]
    blocks_here, rows = in_refs[0].shape[:2]
    for block in range(blocks_here):
        total = in_refs[0][block]
        for ref in in_refs[1:]:
            total = total + ref[block]
        out_ref[pl.ds(block, rows, stride=blocks_here), :] = total


def mesh_kernel(columns, back_groups, blocks_here, *refs):
    sides = PLANE - 1
    ids_ref, weights_ref, source_ref, cotangent_ref = refs[:4]
    rest = refs[4:]
    unit_refs, rest = rest[: 2 * columns], rest[2 * columns :]
    near_refs, rest = rest[: 2 * sides], rest[2 * sides :]
    side_in = None
    if columns > 1:
        side_in, rest = rest[:sides], rest[sides:]
    fields_ref, own_out = rest[:2]
    rest = rest[2:]
    side_out = rest[: len(back_groups) * sides]
    history, magnetic, keep, picked, sums, entry_of, in_sem, out_sem = rest[
        len(back_groups) * sides :
    ]

    meshes = source_ref.shape[0]
    layers, height, width = source_ref.shape[2:]
    entries = 2 * layers
    slots = history.shape[0]
    rows = PARTS * height
    me = lax.axis_index("dev")

    def incoming(mesh, slot):
        return [
            pltpu.make_async_copy(ref.at[mesh], history.at[slot, run, 0], in_sem.at[slot, run])
            for run, ref in enumerate((source_ref, cotangent_ref))
        ]

    def outgoing(mesh, slot):
        return pltpu.make_async_copy(
            history.at[slot, 0, STEPS], fields_ref.at[mesh], out_sem.at[slot]
        )

    for mesh in range(slots):
        for copy in incoming(mesh, mesh):
            copy.start()

    def note_entries(mesh, carry):
        for entry in range(entries):
            owner, _ = split_block(ids_ref[mesh, entry], blocks_here)
            entry_of[owner] = mesh * entries + entry
        return carry

    lax.fori_loop(0, meshes, note_entries, 0)

    def place_of(column, side, core):
        entry = entry_of[me ^ offset(column, side, core)]
        mesh = lax.div(entry, entries)
        inner = entry - mesh * entries
        far = inner >= layers
        layer = jnp.where(far, inner - layers, inner)
        fraction = weights_ref[mesh, layer].astype(jnp.float32) * 0.125
        return entry, mesh, inner, layer, jnp.where(far, 1.0 - fraction, fraction)

    for column in range(columns):
        for core in range(2):
            for side in range(PLANE):
                entry, mesh, inner, _, share = place_of(column, side, core)
                if side and column:
                    values = side_in[side - 1][2 * (column - 1) + core]
                else:
                    _, row = split_block(ids_ref[mesh, inner], blocks_here)
                    dense = near_refs[2 * (side - 1) + core] if side else unit_refs[2 * column + core]
                    values = dense[pl.ds(row, rows, stride=blocks_here), :]
                picked[entry] = share * values

    lane = lax.broadcasted_iota(jnp.int32, (height, width), 1)
    line = lax.broadcasted_iota(jnp.int32, (height, width), 0)
    last_lane, first_lane = lane == width - 1, lane == 0
    last_line, first_line = line == height - 1, line == 0

    def plus_z(v):
        return jnp.where(last_lane, 0.0, pltpu.roll(v, width - 1, 1)) - v

    def plus_y(v):
        return jnp.where(last_line, 0.0, pltpu.roll(v, height - 1, 0)) - v

    def minus_z(v):
        return v - jnp.where(first_lane, 0.0, pltpu.roll(v, 1, 1))

    def minus_y(v):
        return v - jnp.where(first_line, 0.0, pltpu.roll(v, 1, 0))

    def sweep(slot, step, runs):
        for run in runs:
            now = [history[slot, run, step, c, 0] for c in range(PARTS)]
            below = None
            for layer in range(layers):
                ex, ey, ez = now
                if layer + 1 < layers:
                    above = [history[slot, run, step, c, layer + 1] for c in range(PARTS)]
                    dx_y, dx_z = above[1] - ey, above[2] - ez
                else:
                    above = None
                    dx_y, dx_z = -ey, -ez
                gx = magnetic[run, 0, layer] - 0.25 * (plus_y(ez) - plus_z(ey))
                gy = magnetic[run, 1, layer] - 0.25 * (plus_z(ex) - dx_z)
                gz = magnetic[run, 2, layer] - 0.25 * (dx_y - plus_y(ex))
                magnetic[run, 0, layer] = gx
                magnetic[run, 1, layer] = gy
                magnetic[run, 2, layer] = gz
                if below is None:
                    bx_y, bx_z = gy, gz
                else:
                    bx_y, bx_z = gy - below[0], gz - below[1]
                below = (gy, gz)
                history[slot, run, step + 1, 0, layer] = keep[0, layer] * ex + (
                    minus_y(gz) - minus_z(gy)
                )
                history[slot, run, step + 1, 1, layer] = keep[1, layer] * ey + (
                    minus_z(gx) - bx_z
                )
                history[slot, run, step + 1, 2, layer] = keep[2, layer] * ez + (
                    bx_y - minus_y(gx)
                )
                now = above

    def one_mesh(mesh, carry):
        slot = lax.rem(mesh, slots)
        for layer in range(layers):
            near = mesh * entries + layer
            for c in range(PARTS):
                lines = pl.ds(c * height, height)
                keep[c, layer] = 1.0 - 0.5 * (picked[near, lines] + picked[near + layers, lines])
        magnetic[...] = jnp.zeros_like(magnetic)
        for copy in incoming(mesh, slot):
            copy.wait()

        @pl.when(mesh >= slots)
        def _():
            outgoing(mesh - slots, slot).wait()

        def step_of(step, inner):
            sweep(slot, step, (0, 1))
            return inner

        lax.fori_loop(0, STEPS - 1, step_of, 0)
        sweep(slot, STEPS - 1, (0,))
        outgoing(mesh, slot).start()
        for layer in range(layers):
            for c in range(PARTS):
                total = None
                for step in range(STEPS):
                    term = (
                        history[slot, 0, step, c, layer]
                        * history[slot, 1, STEPS - 1 - step, c, layer]
                    )
                    total = term if total is None else total + term
                sums[mesh * layers + layer, c * height : (c + 1) * height] = -0.5 * total

        @pl.when(mesh + slots < meshes)
        def _():
            for copy in incoming(mesh + slots, slot):
                copy.start()

        return carry

    lax.fori_loop(0, meshes, one_mesh, 0)

    for which, group in enumerate(back_groups):
        for place, column in enumerate(group):
            for core in range(2):
                for side in range(PLANE):
                    _, mesh, _, layer, share = place_of(column, side, core)
                    values = share * sums[mesh * layers + layer]
                    if side == 0:
                        own_out[2 * column + core] = values
                    else:
                        side_out[which * sides + side - 1][2 * place + core] = values
    for mesh in range(meshes - slots, meshes):
        outgoing(mesh, mesh % slots).wait()


def local(conductivity, block_ids, weights, source, cotangent):
    blocks_here, _, cells = conductivity.shape
    meshes, _, layers, height, width = source.shape
    count = lax.axis_size("dev")
    rows = PARTS * cells // width
    columns = count // (2 * PLANE)
    back_groups = stages(columns)
    sides = range(1, PLANE)
    f32 = jnp.float32
    slow = pl.CostEstimate(flops=0, transcendentals=0, bytes_accessed=1 << 25)

    def swap(value, bits):
        return lax.ppermute(value, "dev", [(i, i ^ bits) for i in range(count)])

    def shape(*dims):
        return jax.ShapeDtypeStruct(dims, f32)

    own = conductivity.reshape(blocks_here, rows, width).transpose(1, 0, 2).reshape(-1, width)
    units = {(column, 0): swap(own, offset(column, 0, 0)) for column in range(columns - 1, 0, -1)}
    units[0, 0] = own
    near = {(side, 0): swap(own, offset(0, side, 0)) for side in sides}
    peer_ids = [swap(block_ids, offset(0, side, 0)) for side in sides]
    for column in range(columns):
        units[column, 1] = swap(units[column, 0], 1)
    for side in sides:
        near[side, 1] = swap(near[side, 0], 1)
    table = pl.pallas_call(
        functools.partial(lookup_kernel, columns, blocks_here),
        out_shape=jax.ShapeDtypeStruct((PLANE, 2 * columns), jnp.int32),
        in_specs=[SMEM] * PLANE,
        out_specs=SMEM,
        scratch_shapes=[pltpu.SMEM((PLANE, count), jnp.int32)],
        compiler_params=limit(16),
        cost_estimate=slow,
        name="lookup",
    )(block_ids, *peer_ids)
    side_in = []
    far = tuple(range(1, columns))
    if far:
        picked = pl.pallas_call(
            functools.partial(gather_kernel, far, blocks_here),
            out_shape=[shape(2 * len(far), rows, width)] * len(sides),
            in_specs=[SMEM] + [VMEM] * (2 * len(far)),
            out_specs=[VMEM] * len(sides),
            compiler_params=limit(16),
            cost_estimate=slow,
            name="collect",
        )(table, *(units[column, core] for column in far for core in range(2)))
        side_in = [swap(value, offset(0, side, 0)) for side, value in zip(sides, picked)]

    slots = min(meshes, 2)
    fields, own_rows, *side_rows = pl.pallas_call(
        functools.partial(mesh_kernel, columns, back_groups, blocks_here),
        out_shape=[shape(*source.shape), shape(2 * columns, rows, width)]
        + [shape(2 * len(group), rows, width) for group in back_groups for _ in sides],
        in_specs=[SMEM, SMEM, HBM, HBM] + [VMEM] * (2 * columns + len(near) + len(side_in)),
        out_specs=[HBM] + [VMEM] * (1 + len(back_groups) * len(sides)),
        scratch_shapes=[
            pltpu.VMEM((slots, 2, STEPS + 1, PARTS, layers, height, width), f32),
            pltpu.VMEM((2, PARTS, layers, height, width), f32),
            pltpu.VMEM((PARTS, layers, height, width), f32),
            pltpu.VMEM((count, rows, width), f32),
            pltpu.VMEM((meshes * layers, rows, width), f32),
            pltpu.SMEM((count,), jnp.int32),
            pltpu.SemaphoreType.DMA((slots, 2)),
            pltpu.SemaphoreType.DMA((slots,)),
        ],
        compiler_params=limit(40),
        name="leapfrog",
    )(
        block_ids,
        weights,
        source,
        cotangent,
        *(units[column, core] for column in range(columns) for core in range(2)),
        *(near[side, core] for side in sides for core in range(2)),
        *side_in,
    )

    returned = {}
    for which, group in enumerate(back_groups):
        pieces = side_rows[which * len(sides) : (which + 1) * len(sides)]
        arrived = [swap(value, offset(0, side, 0)) for side, value in zip(sides, pieces)]
        operands = (table, own_rows, *arrived)
        specs = [SMEM] + [VMEM] * (1 + len(sides))
        partner = pl.pallas_call(
            functools.partial(partner_kernel, group, 1),
            out_shape=shape(len(group), blocks_here, rows, width),
            in_specs=specs,
            out_specs=VMEM,
            compiler_params=limit(16),
            name="partner",
        )(*operands)
        partner = swap(partner, 1)
        totals = pl.pallas_call(
            functools.partial(partner_kernel, group, 0),
            out_shape=[shape(blocks_here, rows, width)] * len(group),
            in_specs=specs + [VMEM],
            out_specs=[VMEM] * len(group),
            compiler_params=limit(16),
            name="column",
        )(*operands, partner)
        for column, total in zip(group, totals):
            returned[column] = swap(total, offset(column, 0, 0)) if column else total
    gradient = pl.pallas_call(
        final_kernel,
        out_shape=shape(rows * blocks_here, width),
        in_specs=[VMEM] * columns,
        out_specs=VMEM,
        compiler_params=limit(16),
        name="total",
    )(*(returned[column] for column in range(columns)))
    gradient = gradient.reshape(rows, blocks_here, width).transpose(1, 0, 2)
    return fields, gradient.reshape(conductivity.shape)


def stages(columns):
    return [group for group in (tuple(range(1, columns)), (0,)) if group]


def solution(mesh):
    placed = (
        P("dev", None, None),
        P("dev", None),
        P("dev", None),
        P("dev", None, None, None, None),
        P("dev", None, None, None, None),
    )

    return jax.shard_map(
        local,
        mesh=mesh,
        in_specs=placed,
        out_specs=(P("dev", None, None, None, None), P("dev", None, None)),
        check_vma=False,
    )
```
